32 devices in a mesh: wide: 8 (over z, x), narrow: 4 (over y, core).
Axes of the slice: x: 2, y: 2, z: 4, core: 2. Of those that a mesh axis runs over, the one named last changes fastest.
Arguments:
- density: bfloat16 [4096, 4096], P('wide', 'narrow'), may hold values from -0.0059814453 to 0.0059814453
- block_slot: int32 [32], replicated, may hold values from 0 to 31, as said below
- region_blocks: int32 [512], P(('wide', 'narrow')), may hold values from 0 to 31, as said below
- basis_lists: int32 [384, 8], P(('wide', 'narrow')), may hold values from 0 to 15, as said below
- point_counts: int32 [384], P(('wide', 'narrow')), may hold values from 1 to 256
- orbitals: bfloat16 [384, 1024, 256], P(('wide', 'narrow')), may hold values from -6 to 6
- weights: float32 [384, 256], P(('wide', 'narrow')), may hold values from 0.01 to 0.1
- harmonics: bfloat16 [384, 64, 256], P(('wide', 'narrow')), may hold values from -32 to 32
Outputs:
- hamiltonian: float32 [4096, 4096], P('wide', 'narrow')
The draws below stay inside these ranges and needn't reach their ends.
Inputs may be any that keep to these rules, and one draw needn't show every extreme that they name: `block_slot`: a permutation of the 32 layout slots. `region_blocks`: the 16 blocks of one region are distinct; among the 256 block pairs of one region, no owner of the layout holds more than 8, and some owner holds exactly 8. `basis_lists`: the 8 positions of one list are distinct.
All inputs are finite; a program needn't handle non-finite values.
Results may differ from the reference program's by a relative error of at most 0.0023.
Values may be sent and summed in bfloat16 or wider, within the bound.
A program may use at most 128 MiB of HBM per device.

```python
import math
import jax
import jax.numpy as jnp
from jax import lax

BLK = 128
PTS = 256
K = 8
S = 16
NL = 64
QB = 4
BATCH_DEV = 12
NB = 32
BATCHES = 384
TOTAL_PTS = 98304
N_WIDE = 8
N_NARROW = 4


def slot_table(key):
    return jax.random.permutation(jax.random.fold_in(key, 11), NB).astype(jnp.int32)


def draw_block_slot(key, part):
    return slot_table(key)


def draw_region_blocks(key, part):
    devices_all = N_WIDE * N_NARROW
    table = slot_table(key)
    inverse = jnp.argsort(table).astype(jnp.int32)
    starts = jax.random.randint(jax.random.fold_in(key, 12), (devices_all,), 0, N_WIDE)
    offsets = jnp.arange(S)
    residue = (starts[:, None] + offsets[None, :]) % N_WIDE
    q_pick = jax.random.randint(jax.random.fold_in(key, 13), (devices_all, N_WIDE), 0, QB)
    q_base = q_pick[:, offsets % N_WIDE]
    q_value = (q_base + (offsets // N_WIDE)[None, :]) % QB
    slots = q_value * N_WIDE + residue
    return inverse[slots].reshape(-1).astype(jnp.int32)


def draw_basis_lists(key, part):
    scores = jax.random.randint(jax.random.fold_in(key, 21), (BATCHES, S), 0, 1048576)
    scores = scores * S + jnp.arange(S)[None, :]
    order = jnp.argsort(scores, axis=1)
    return order[:, :K].astype(jnp.int32)


def draw_point_counts(key, part):
    devices_all = N_WIDE * N_NARROW
    levels = jax.random.randint(jax.random.fold_in(key, 31), (devices_all,), 1, 5)
    chosen = jax.random.randint(jax.random.fold_in(key, 32), (), 0, devices_all)
    levels = jnp.where(jnp.arange(devices_all) == chosen, 4, levels)
    limits = PTS * levels // 4
    device_of = jnp.arange(BATCHES) // BATCH_DEV
    batch_of = jnp.arange(BATCHES) % BATCH_DEV
    limit_row = limits[device_of]
    raw = jax.random.randint(jax.random.fold_in(key, 33), (BATCHES,), 0, PTS)
    counts = 1 + raw % limit_row
    return jnp.where(batch_of == 0, limit_row, counts).astype(jnp.int32)


def draw_harmonics(key, part):
    devices_all = N_WIDE * N_NARROW
    device_of = (jnp.arange(BATCHES) // BATCH_DEV).astype(jnp.float32)
    ramp = 1.0 + 2.0 * device_of / max(devices_all - 1, 1)
    base = jnp.clip(jax.random.normal(key, (BATCHES, NL, PTS), jnp.float32), -4.0, 4.0)
    values = base * ramp[:, None, None]
    return values.astype(jnp.bfloat16)


def level_of(own_key, dims, shards, low, top_value):
    gain, own = 1.0, jax.random.fold_in(own_key, 6)
    for position, shards_of in shards:
        steps = jnp.exp(jax.random.uniform(jax.random.fold_in(own, position), (shards_of,), jnp.float32, low / len(shards), top_value / len(shards)))
        gain = gain * jnp.repeat(steps, dims[position] // shards_of).reshape([-1 if axis == position else 1 for axis in range(len(dims))])
    return gain


def normal_values(stream_key, extent, spread, bound, pieces=(), held_as=jnp.bfloat16):
    values = jax.random.normal(stream_key, extent, jnp.float32) * spread
    if len(pieces) > 0:
        values = level_of(stream_key, extent, pieces, -0.22, 0.18) * values
    return jnp.clip(values, min=-bound, max=bound).astype(held_as)


def setup_inputs(seed: int = 0) -> dict:
    keys = jax.random.split(jax.random.key(seed), 9)
    return {
        "density": normal_values(keys[0], (NB * BLK, NB * BLK), 0.001, 0.0059814453, ((0, 8), (1, 4))),
        "block_slot": draw_block_slot(jax.random.fold_in(keys[8], 71), 0),
        "region_blocks": draw_region_blocks(jax.random.fold_in(keys[8], 71), 0),
        "basis_lists": draw_basis_lists(jax.random.fold_in(keys[8], 71), 0),
        "point_counts": draw_point_counts(jax.random.fold_in(keys[8], 71), 0),
        "orbitals": normal_values(keys[5], (BATCHES, K * BLK, PTS), 1.0, 6.0, ((0, 32),)),
        "weights": jnp.clip(jnp.exp(math.log(0.1) - 2.3025851 * jax.random.uniform(keys[6], (BATCHES, PTS), jnp.float32) ** level_of(keys[6], (BATCHES, PTS), ((0, 32),), -0.2, 0.2)), 0.01, 0.1),
        "harmonics": draw_harmonics(jax.random.fold_in(keys[8], 71), 0),
    }


FAR_COEFF = 10.0

def layout_positions(slots):
    col_blocks = NB // N_NARROW
    row_index = slots % N_WIDE * QB + slots // N_WIDE
    col_index = slots % N_NARROW * col_blocks + slots // N_NARROW
    return (row_index, col_index)

def reference(density, block_slot, region_blocks, basis_lists, point_counts, orbitals, weights, harmonics):
    devices_all = N_WIDE * N_NARROW
    slots = block_slot[region_blocks].reshape(devices_all, S)
    row_index, col_index = layout_positions(slots)
    blocks_four = density.reshape(NB, BLK, NB, BLK)
    lists_all = basis_lists.reshape(devices_all, BATCH_DEV, K)
    orbs_all = orbitals.reshape(devices_all, BATCH_DEV, K, BLK, PTS)

    def device_density(packed):
        rows_dev, cols_dev, lists_dev, orbs_dev = packed
        region = blocks_four[rows_dev[:, None], :, cols_dev[None, :], :].astype(jnp.float32)

        def batch_density(inner):
            list_row, orb_rows = inner
            sub_matrix = region[list_row[:, None], list_row[None, :]]
            orb_float = orb_rows.astype(jnp.float32)
            product = jnp.einsum('acij,cjp->aip', sub_matrix, orb_float, precision=lax.Precision.HIGHEST)
            return lax.optimization_barrier(jnp.sum(product * orb_float, axis=(0, 1)))
        return lax.map(batch_density, (lists_dev, orbs_dev))
    dens_pts = lax.map(device_density, (row_index, col_index, lists_all, orbs_all)).reshape(BATCHES, PTS)
    live_mask = jnp.arange(PTS)[None, :] < point_counts[:, None]
    live_weight = jnp.where(live_mask, weights, jnp.float32(0.0))
    harm_float = harmonics.astype(jnp.float32)
    moments = lax.optimization_barrier(jnp.sum((live_weight * dens_pts)[:, None, :] * harm_float, axis=(0, 2)))
    far_field = FAR_COEFF * lax.optimization_barrier(jnp.sum(moments[None, :, None] * harm_float, axis=1)) / math.sqrt(TOTAL_PTS * NL)
    potential = 0.5 * dens_pts - (1.0 + dens_pts * dens_pts) ** (1.0 / 6.0) + far_field
    factor = live_weight * potential
    orb_four = orbitals.reshape(BATCHES, K, BLK, PTS)
    scaled = lax.optimization_barrier((orb_four.astype(jnp.float32) * factor[:, None, None, :]).astype(jnp.bfloat16))
    scaled_all = scaled.reshape(devices_all, BATCH_DEV, K, BLK, PTS)

    def add_device(total, packed):
        rows_dev, cols_dev, lists_dev, scaled_dev, orbs_dev = packed

        def add_batch(partial_h, inner):
            list_row, scaled_rows, orb_rows = inner
            term = jnp.einsum('aip,cjp->acij', scaled_rows.astype(jnp.float32), orb_rows.astype(jnp.float32), precision=lax.Precision.HIGHEST)
            return (partial_h.at[list_row[:, None], list_row[None, :]].add(term), None)
        start = jnp.zeros((S, S, BLK, BLK), jnp.float32)
        partial_h = lax.scan(add_batch, start, (lists_dev, scaled_dev, orbs_dev))[0]
        rounded = lax.optimization_barrier(partial_h.astype(jnp.bfloat16)).astype(jnp.float32)
        return (total.at[rows_dev[:, None], :, cols_dev[None, :], :].add(rounded), None)
    total = jnp.zeros((NB, BLK, NB, BLK), jnp.float32)
    total = lax.scan(add_device, total, (row_index, col_index, lists_all, scaled_all, orbs_all))[0]
    return total.reshape(NB * BLK, NB * BLK)
```

```python
import functools
import math

import jax
import jax.numpy as jnp
from jax import lax
from jax.experimental import pallas as pl
from jax.experimental.pallas import tpu as pltpu
from jax.sharding import PartitionSpec as P

BLK = 128
FAR_COEFF = 10.0
RING = 4
LANES = 128
MESH = pl.DeviceIdType.MESH
VMEM_BYTES = 58 * 1024 * 1024


def plane_peer(offset, inner, narrow):
    wide_me = lax.axis_index("wide")
    group = inner * narrow
    base = wide_me // inner * inner
    mine = wide_me % inner * narrow + lax.axis_index("narrow")
    other = lax.rem(mine + offset, group)
    return mine, other, (base + other // narrow, other % narrow)


def plane_barrier(inner, narrow):
    barrier = pltpu.get_barrier_semaphore()
    for offset in range(1, inner * narrow):
        _, _, device = plane_peer(offset, inner, narrow)
        pl.semaphore_signal(barrier, inc=1, device_id=device, device_id_type=MESH)
    pl.semaphore_wait(barrier, inner * narrow - 1)


def tile_kernel(inner, narrow, tile_ref, out_ref, send_sem, recv_sem):
    plane_barrier(inner, narrow)
    copies = []
    for offset in range(1, inner * narrow):
        mine, _, device = plane_peer(offset, inner, narrow)
        copy = pltpu.make_async_remote_copy(
            src_ref=tile_ref,
            dst_ref=out_ref.at[mine],
            send_sem=send_sem.at[offset - 1],
            recv_sem=recv_sem.at[offset - 1],
            device_id=device,
            device_id_type=MESH,
        )
        copy.start()
        copies.append(copy)
    mine, _, _ = plane_peer(0, inner, narrow)
    out_ref[mine] = tile_ref[...]
    for copy in copies:
        copy.wait()


def share_tile(tile, inner, narrow):
    group = inner * narrow
    return pl.pallas_call(
        functools.partial(tile_kernel, inner, narrow),
        out_shape=jax.ShapeDtypeStruct((group,) + tile.shape, tile.dtype),
        in_specs=[pl.BlockSpec(memory_space=pltpu.VMEM)],
        out_specs=pl.BlockSpec(memory_space=pltpu.VMEM),
        scratch_shapes=[
            pltpu.SemaphoreType.DMA((group - 1,)),
            pltpu.SemaphoreType.DMA((group - 1,)),
        ],
        compiler_params=pltpu.CompilerParams(collective_id=0, has_side_effects=True),
        name="share_tile",
    )(tile)


def exchange_kernel(inner, narrow, src_ref, out_ref, own, send_sem, recv_sem, own_sem):
    mine, _, _ = plane_peer(0, inner, narrow)
    take = pltpu.make_async_copy(src_ref.at[mine], own, own_sem.at[0])
    take.start()
    plane_barrier(inner, narrow)
    copies = []
    for offset in range(1, inner * narrow):
        _, other, device = plane_peer(offset, inner, narrow)
        copy = pltpu.make_async_remote_copy(
            src_ref=src_ref.at[other],
            dst_ref=out_ref.at[mine],
            send_sem=send_sem.at[offset - 1],
            recv_sem=recv_sem.at[offset - 1],
            device_id=device,
            device_id_type=MESH,
        )
        copy.start()
        copies.append(copy)
    take.wait()
    put = pltpu.make_async_copy(own, out_ref.at[mine], own_sem.at[1])
    put.start()
    put.wait()
    for copy in copies:
        copy.wait()


def exchange(blocks, inner, narrow):
    group = inner * narrow
    size = math.prod(blocks.shape) * 2
    return pl.pallas_call(
        functools.partial(exchange_kernel, inner, narrow),
        out_shape=jax.ShapeDtypeStruct(blocks.shape, blocks.dtype),
        in_specs=[pl.BlockSpec(memory_space=pl.ANY)],
        out_specs=pl.BlockSpec(memory_space=pl.ANY),
        scratch_shapes=[
            pltpu.VMEM(blocks.shape[1:], blocks.dtype),
            pltpu.SemaphoreType.DMA((group - 1,)),
            pltpu.SemaphoreType.DMA((group - 1,)),
            pltpu.SemaphoreType.DMA((2,)),
        ],
        compiler_params=pltpu.CompilerParams(collective_id=1, has_side_effects=True),
        cost_estimate=pl.CostEstimate(
            flops=0, bytes_accessed=size * 32, transcendentals=0
        ),
        name="exchange",
    )(blocks)


def total_kernel(devices, narrow, tile_ref, out_ref, held, send_sem, recv_sem):
    mine = lax.axis_index("wide") * narrow + lax.axis_index("narrow")

    def device_at(offset):
        other = lax.rem(mine + offset, devices)
        return (other // narrow, other % narrow)

    barrier = pltpu.get_barrier_semaphore()

    def greet(offset, carry):
        pl.semaphore_signal(
            barrier, inc=1, device_id=device_at(offset), device_id_type=MESH
        )
        return carry

    def copy_at(offset):
        return pltpu.make_async_remote_copy(
            src_ref=tile_ref,
            dst_ref=held.at[mine],
            send_sem=send_sem.at[offset - 1],
            recv_sem=recv_sem.at[offset - 1],
            device_id=device_at(offset),
            device_id_type=MESH,
        )

    def send(offset, carry):
        copy_at(offset).start()
        return carry

    def finish(offset, carry):
        copy_at(offset).wait()
        return carry

    lax.fori_loop(1, devices, greet, 0)
    pl.semaphore_wait(barrier, devices - 1)
    lax.fori_loop(1, devices, send, 0)
    held[mine] = tile_ref[...]
    lax.fori_loop(1, devices, finish, 0)
    out_ref[...] = jnp.sum(held[...], axis=0)


def total_over_devices(tile, devices, narrow):
    return pl.pallas_call(
        functools.partial(total_kernel, devices, narrow),
        out_shape=jax.ShapeDtypeStruct(tile.shape, tile.dtype),
        in_specs=[pl.BlockSpec(memory_space=pltpu.VMEM)],
        out_specs=pl.BlockSpec(memory_space=pltpu.VMEM),
        scratch_shapes=[
            pltpu.VMEM((devices,) + tile.shape, tile.dtype),
            pltpu.SemaphoreType.DMA((devices - 1,)),
            pltpu.SemaphoreType.DMA((devices - 1,)),
        ],
        compiler_params=pltpu.CompilerParams(collective_id=2, has_side_effects=True),
        name="total_over_devices",
    )(tile)


def select_kernel(row_cap, col_cap, rows_ref, cols_ref, dens_ref, out_ref):
    dest = pl.program_id(0)
    for rr in range(row_cap):
        row = pl.multiple_of(rows_ref[dest, rr] * BLK, BLK)
        for cr in range(col_cap):
            col = pl.multiple_of(cols_ref[dest, cr] * BLK, BLK)
            out_ref[0, rr * col_cap + cr] = dens_ref[pl.ds(row, BLK), pl.ds(col, BLK)]


def select(dens, rows, cols):
    group, row_cap = rows.shape
    col_cap = cols.shape[1]
    cap = row_cap * col_cap
    return pl.pallas_call(
        functools.partial(select_kernel, row_cap, col_cap),
        out_shape=jax.ShapeDtypeStruct((group, cap, BLK, BLK), dens.dtype),
        grid_spec=pltpu.PrefetchScalarGridSpec(
            num_scalar_prefetch=2,
            grid=(group,),
            in_specs=[pl.BlockSpec(dens.shape, lambda g, *_: (0, 0))],
            out_specs=pl.BlockSpec((1, cap, BLK, BLK), lambda g, *_: (g, 0, 0, 0)),
        ),
        compiler_params=pltpu.CompilerParams(vmem_limit_bytes=VMEM_BYTES),
        name="select",
    )(rows, cols, dens)


def combine_kernel(row_cap, col_cap, has_prev, rows_ref, cols_ref, got_ref, *rest):
    if has_prev:
        prev_ref, out_ref, acc = rest
    else:
        prev_ref, (out_ref, acc) = None, rest
    source = pl.program_id(0)

    @pl.when(source == 0)
    def _():
        if has_prev:
            acc[...] = prev_ref[...].astype(jnp.float32)
        else:
            acc[...] = jnp.zeros_like(acc)

    for rr in range(row_cap):
        row = pl.multiple_of(rows_ref[source, rr] * BLK, BLK)
        for cr in range(col_cap):
            col = pl.multiple_of(cols_ref[source, cr] * BLK, BLK)
            acc[pl.ds(row, BLK), pl.ds(col, BLK)] += got_ref[
                0, rr * col_cap + cr
            ].astype(jnp.float32)

    @pl.when(source == pl.num_programs(0) - 1)
    def _():
        out_ref[...] = acc[...].astype(out_ref.dtype)


def combine(got, prev, rows, cols, shape, dtype):
    group, row_cap = rows.shape
    col_cap = cols.shape[1]
    cap = row_cap * col_cap
    whole = pl.BlockSpec(shape, lambda g, *_: (0, 0))
    specs = [pl.BlockSpec((1, cap, BLK, BLK), lambda g, *_: (g, 0, 0, 0))]
    operands = [got]
    if prev is not None:
        specs.append(whole)
        operands.append(prev)
    return pl.pallas_call(
        functools.partial(combine_kernel, row_cap, col_cap, prev is not None),
        out_shape=jax.ShapeDtypeStruct(shape, dtype),
        grid_spec=pltpu.PrefetchScalarGridSpec(
            num_scalar_prefetch=2,
            grid=(group,),
            in_specs=specs,
            out_specs=whole,
            scratch_shapes=[pltpu.VMEM(shape, jnp.float32)],
        ),
        compiler_params=pltpu.CompilerParams(vmem_limit_bytes=VMEM_BYTES),
        name="combine",
    )(rows, cols, *operands)


def live_row(weights_ref, counts_ref, batch):
    points = weights_ref.shape[1]
    point = lax.broadcasted_iota(jnp.int32, (1, points), 1)
    return jnp.where(
        point < counts_ref[batch], weights_ref[pl.ds(batch, 1), :], jnp.float32(0.0)
    )


def density_kernel(
    steps, list_len, lists_ref, row_ref, col_ref, counts_ref, orb_ref, harm_ref, weights_ref, *rest
):
    chunks = rest[:steps]
    rho_ref, moment_ref, held, matrix, sems = rest[steps:]
    batch = pl.program_id(0)
    per_chunk = held.shape[0] // steps

    @pl.when(batch == 0)
    def _():
        copies = [
            pltpu.make_async_copy(
                chunks[k], held.at[pl.ds(k * per_chunk, per_chunk)], sems.at[k]
            )
            for k in range(steps)
        ]
        for copy in copies:
            copy.start()
        moment_ref[...] = jnp.zeros_like(moment_ref)
        for copy in copies:
            copy.wait()

    places = [lists_ref[batch, k] for k in range(list_len)]
    cols = [col_ref[place] for place in places]
    for k in range(list_len):
        row = row_ref[places[k]]
        for k2 in range(list_len):
            matrix[k * BLK : (k + 1) * BLK, k2 * BLK : (k2 + 1) * BLK] = held[row + cols[k2]]
    orbs = orb_ref[0]
    rows_each = 2 * BLK
    total = jnp.zeros((1, orbs.shape[1]), jnp.float32)
    for top in range(0, list_len * BLK, rows_each):
        product = jnp.dot(
            matrix[top : top + rows_each, :], orbs, preferred_element_type=jnp.float32
        )
        part = product * orb_ref[0, top : top + rows_each, :].astype(jnp.float32)
        total += jnp.sum(part, axis=0, keepdims=True)
    rho_ref[pl.ds(batch, 1), :] = total
    live = live_row(weights_ref, counts_ref, batch) * total
    moment_ref[...] += harm_ref[0].astype(jnp.float32) * live


def density_points(lists, rows, cols, counts, orbitals, harmonics, weights, chunks):
    batches, height, points = orbitals.shape
    list_len = lists.shape[1]
    components = harmonics.shape[1]
    steps = len(chunks)
    blocks = [chunk.reshape(-1, BLK, BLK) for chunk in chunks]
    held = steps * blocks[0].shape[0]
    full = lambda shape: pl.BlockSpec(shape, lambda g, *_: (0, 0))
    return pl.pallas_call(
        functools.partial(density_kernel, steps, list_len),
        out_shape=[
            jax.ShapeDtypeStruct((batches, points), jnp.float32),
            jax.ShapeDtypeStruct((components, points), jnp.float32),
        ],
        grid_spec=pltpu.PrefetchScalarGridSpec(
            num_scalar_prefetch=4,
            grid=(batches,),
            in_specs=[
                pl.BlockSpec((1, height, points), lambda g, *_: (g, 0, 0)),
                pl.BlockSpec((1, components, points), lambda g, *_: (g, 0, 0)),
                full((batches, points)),
            ]
            + [pl.BlockSpec(memory_space=pl.ANY)] * steps,
            out_specs=[full((batches, points)), full((components, points))],
            scratch_shapes=[
                pltpu.VMEM((held, BLK, BLK), jnp.bfloat16),
                pltpu.VMEM((height, height), jnp.bfloat16),
                pltpu.SemaphoreType.DMA((steps,)),
            ],
        ),
        compiler_params=pltpu.CompilerParams(vmem_limit_bytes=VMEM_BYTES),
        name="density_points",
    )(lists, rows, cols, counts, orbitals, harmonics, weights, *blocks)


def integral_kernel(
    steps,
    list_len,
    far_scale,
    lists_ref,
    row_ref,
    col_ref,
    counts_ref,
    orb_ref,
    harm_ref,
    weights_ref,
    rho_ref,
    moment_ref,
    *rest,
):
    outs = rest[:steps]
    acc, stage, sems = rest[steps:]
    batch = pl.program_id(0)
    per_chunk = acc.shape[0] // steps

    @pl.when(batch == 0)
    def _():
        @pl.loop(0, acc.shape[0])
        def _(place):
            acc[place] = jnp.zeros(acc.shape[1:], jnp.float32)

    rho = rho_ref[pl.ds(batch, 1), :]
    far = FAR_COEFF * jnp.sum(
        moment_ref[...] * harm_ref[0].astype(jnp.float32), axis=0, keepdims=True
    )
    sixth = jnp.exp(jnp.log(1.0 + rho * rho) * (1.0 / 6.0))
    potential = 0.5 * rho - sixth + far / far_scale
    factor = live_row(weights_ref, counts_ref, batch) * potential
    orbs = orb_ref[0]
    scaled = (orbs.astype(jnp.float32) * factor).astype(jnp.bfloat16)
    places = [lists_ref[batch, k] for k in range(list_len)]
    rows = [row_ref[place] for place in places]
    cols = [col_ref[place] for place in places]
    for pair in range(0, list_len, 2):
        right = orb_ref[0, pair * BLK : (pair + 2) * BLK, :]
        term = lax.dot_general(
            scaled, right, (((1,), (1,)), ((), ())), preferred_element_type=jnp.float32
        )
        for k in range(list_len):
            for k2 in range(2):
                acc[rows[k] + cols[pair + k2]] += term[
                    k * BLK : (k + 1) * BLK, k2 * BLK : (k2 + 1) * BLK
                ]

    @pl.when(batch == pl.num_programs(0) - 1)
    def _():
        copies = []
        for k in range(steps):
            if k >= 2:
                copies[k - 2].wait()

            @pl.loop(0, per_chunk)
            def _(place, k=k):
                stage[k % 2, place] = acc[k * per_chunk + place].astype(jnp.bfloat16)

            copy = pltpu.make_async_copy(stage.at[k % 2], outs[k], sems.at[k])
            copy.start()
            copies.append(copy)
        for copy in copies[-2:]:
            copy.wait()


def integrals(lists, rows, cols, counts, orbitals, harmonics, weights, rho, moments, steps, held, far_scale):
    batches, height, points = orbitals.shape
    list_len = lists.shape[1]
    components = harmonics.shape[1]
    per_chunk = held // steps
    full = lambda shape: pl.BlockSpec(shape, lambda g, *_: (0, 0))
    return pl.pallas_call(
        functools.partial(integral_kernel, steps, list_len, far_scale),
        out_shape=[jax.ShapeDtypeStruct((per_chunk, BLK, BLK), jnp.bfloat16)] * steps,
        grid_spec=pltpu.PrefetchScalarGridSpec(
            num_scalar_prefetch=4,
            grid=(batches,),
            in_specs=[
                pl.BlockSpec((1, height, points), lambda g, *_: (g, 0, 0)),
                pl.BlockSpec((1, components, points), lambda g, *_: (g, 0, 0)),
                full((batches, points)),
                full((batches, points)),
                full((components, 1)),
            ],
            out_specs=[pl.BlockSpec(memory_space=pl.ANY)] * steps,
            scratch_shapes=[
                pltpu.VMEM((held, BLK, BLK), jnp.float32),
                pltpu.VMEM((2, per_chunk, BLK, BLK), jnp.bfloat16),
                pltpu.SemaphoreType.DMA((steps,)),
            ],
        ),
        compiler_params=pltpu.CompilerParams(vmem_limit_bytes=VMEM_BYTES),
        name="integrals",
    )(lists, rows, cols, counts, orbitals, harmonics, weights, rho, moments)


def rank_among(keys):
    count = keys.shape[0]
    order = jnp.arange(count)
    same = (keys[:, None] == keys[None, :]) & (order[None, :] < order[:, None])
    return jnp.sum(same.astype(jnp.int32), axis=1)


def spread(positions, values, size):
    hit = positions[None, :] == jnp.arange(size)[:, None]
    return jnp.sum(jnp.where(hit, values[None, :], 0), axis=1)


def per_device(
    region, density, block_slot, region_blocks, basis_lists, point_counts, orbitals, weights, harmonics
):
    wide = lax.axis_size("wide")
    narrow = lax.axis_size("narrow")
    devices = wide * narrow
    steps = math.gcd(wide, RING)
    inner = wide // steps
    group = inner * narrow
    row_cap = max(1, region // wide)
    col_cap = region // narrow
    cap = row_cap * col_cap
    wide_me = lax.axis_index("wide")
    narrow_me = lax.axis_index("narrow")
    ring_me = wide_me // inner
    inner_me = wide_me % inner

    known = block_slot.shape[0]
    hit = region_blocks[:, None] == jnp.arange(known)[None, :]
    slots = jnp.sum(jnp.where(hit, block_slot[None, :], 0), axis=1)
    row_owner, row_local = slots % wide, slots // wide
    col_owner, col_local = slots % narrow, slots // narrow
    row_rank, col_rank = rank_among(row_owner), rank_among(col_owner)
    row_table = spread(row_owner * row_cap + row_rank, row_local, LANES)
    col_table = spread(col_owner * col_cap + col_rank, col_local, LANES)
    tile = jnp.concatenate(
        [row_table[None], col_table[None], jnp.zeros((6, LANES), jnp.int32)], axis=0
    )
    tables = share_tile(tile, inner, narrow)
    want_cols = lax.dynamic_slice_in_dim(tables[:, 1], narrow_me * col_cap, col_cap, axis=1)

    def want_rows(ring):
        owner = ring * inner + inner_me
        return lax.dynamic_slice_in_dim(tables[:, 0], owner * row_cap, row_cap, axis=1)

    forward = [(w, (w + inner) % wide) for w in range(wide)]
    chunks = []
    raw = density
    for step in range(steps):
        following = lax.ppermute(raw, "wide", forward) if step < steps - 1 else None
        ring = (ring_me - step + steps) % steps
        chosen = select(raw, want_rows(ring), want_cols)
        chunks.append(exchange(chosen, inner, narrow))
        raw = following

    col_place = col_owner * cap + col_rank
    in_plane = row_owner % inner * (narrow * cap) + row_rank * col_cap
    owner_ring = row_owner // inner
    row_in = (ring_me - owner_ring + steps) % steps * (group * cap) + in_plane
    row_out = (ring_me - 1 - owner_ring + 2 * steps) % steps * (group * cap) + in_plane

    rho, moment_parts = density_points(
        basis_lists, row_in, col_place, point_counts, orbitals, harmonics, weights, chunks
    )
    components = harmonics.shape[1]
    local = jnp.sum(moment_parts, axis=1)
    tile = jnp.zeros((8, LANES), jnp.float32).at[0, :components].set(local)
    moments = total_over_devices(tile, devices, narrow)[0, :components].reshape(components, 1)

    total_points = orbitals.shape[0] * orbitals.shape[2] * devices
    parts = integrals(
        basis_lists,
        row_out,
        col_place,
        point_counts,
        orbitals,
        harmonics,
        weights,
        rho,
        moments,
        steps,
        steps * group * cap,
        math.sqrt(total_points * components),
    )
    running = None
    for step in range(steps):
        got = exchange(parts[step].reshape(group, cap, BLK, BLK), inner, narrow)
        ring = (ring_me - 1 - step + 2 * steps) % steps
        last = step == steps - 1
        running = combine(
            got,
            running,
            want_rows(ring),
            want_cols,
            density.shape,
            jnp.float32 if last else jnp.bfloat16,
        )
        if not last:
            running = lax.ppermute(running, "wide", forward)
    return running


def solution(mesh):
    devices = mesh.shape["wide"] * mesh.shape["narrow"]

    def whole(density, block_slot, region_blocks, *others):
        region = region_blocks.shape[0] // devices
        in_specs = (
            P("wide", "narrow"),
            P(),
            P(("wide", "narrow")),
            P(("wide", "narrow"), None),
            P(("wide", "narrow")),
            P(("wide", "narrow"), None, None),
            P(("wide", "narrow"), None),
            P(("wide", "narrow"), None, None),
        )
        mapped = jax.shard_map(
            functools.partial(per_device, region),
            mesh=mesh,
            in_specs=in_specs,
            out_specs=P("wide", "narrow"),
            check_vma=False,
        )
        return mapped(density, block_slot, region_blocks, *others)

    return whole
```

```python
import functools
import math

import jax
import jax.numpy as jnp
from jax import lax
from jax.experimental import pallas as pl
from jax.experimental.pallas import tpu as pltpu
from jax.sharding import PartitionSpec as P

BLK = 128
FAR_COEFF = 10.0
RING = 4
LANES = 128
MESH = pl.DeviceIdType.MESH
VMEM_BYTES = 58 * 1024 * 1024


def plane_peer(offset, inner, narrow):
    wide_me = lax.axis_index("wide")
    group = inner * narrow
    base = wide_me // inner * inner
    mine = wide_me % inner * narrow + lax.axis_index("narrow")
    other = lax.rem(mine + offset, group)
    return mine, other, (base + other // narrow, other % narrow)


def plane_barrier(inner, narrow):
    barrier = pltpu.get_barrier_semaphore()
    for offset in range(1, inner * narrow):
        _, _, device = plane_peer(offset, inner, narrow)
        pl.semaphore_signal(barrier, inc=1, device_id=device, device_id_type=MESH)
    pl.semaphore_wait(barrier, inner * narrow - 1)


def tile_kernel(inner, narrow, tile_ref, out_ref, send_sem, recv_sem):
    plane_barrier(inner, narrow)
    copies = []
    for offset in range(1, inner * narrow):
        mine, _, device = plane_peer(offset, inner, narrow)
        copy = pltpu.make_async_remote_copy(
            src_ref=tile_ref,
            dst_ref=out_ref.at[mine],
            send_sem=send_sem.at[offset - 1],
            recv_sem=recv_sem.at[offset - 1],
            device_id=device,
            device_id_type=MESH,
        )
        copy.start()
        copies.append(copy)
    mine, _, _ = plane_peer(0, inner, narrow)
    out_ref[mine] = tile_ref[...]
    for copy in copies:
        copy.wait()


def share_tile(tile, inner, narrow):
    group = inner * narrow
    return pl.pallas_call(
        functools.partial(tile_kernel, inner, narrow),
        out_shape=jax.ShapeDtypeStruct((group,) + tile.shape, tile.dtype),
        in_specs=[pl.BlockSpec(memory_space=pltpu.VMEM)],
        out_specs=pl.BlockSpec(memory_space=pltpu.VMEM),
        scratch_shapes=[
            pltpu.SemaphoreType.DMA((group - 1,)),
            pltpu.SemaphoreType.DMA((group - 1,)),
        ],
        compiler_params=pltpu.CompilerParams(collective_id=0, has_side_effects=True),
        name="share_tile",
    )(tile)


def total_kernel(devices, narrow, tile_ref, out_ref, held, send_sem, recv_sem):
    mine = lax.axis_index("wide") * narrow + lax.axis_index("narrow")

    def device_at(offset):
        other = lax.rem(mine + offset, devices)
        return (other // narrow, other % narrow)

    barrier = pltpu.get_barrier_semaphore()

    def greet(offset, carry):
        pl.semaphore_signal(
            barrier, inc=1, device_id=device_at(offset), device_id_type=MESH
        )
        return carry

    def copy_at(offset):
        return pltpu.make_async_remote_copy(
            src_ref=tile_ref,
            dst_ref=held.at[mine],
            send_sem=send_sem.at[offset - 1],
            recv_sem=recv_sem.at[offset - 1],
            device_id=device_at(offset),
            device_id_type=MESH,
        )

    def send(offset, carry):
        copy_at(offset).start()
        return carry

    def finish(offset, carry):
        copy_at(offset).wait()
        return carry

    lax.fori_loop(1, devices, greet, 0)
    pl.semaphore_wait(barrier, devices - 1)
    lax.fori_loop(1, devices, send, 0)
    held[mine] = tile_ref[...]
    lax.fori_loop(1, devices, finish, 0)
    out_ref[...] = jnp.sum(held[...], axis=0)


def total_over_devices(tile, devices, narrow):
    return pl.pallas_call(
        functools.partial(total_kernel, devices, narrow),
        out_shape=jax.ShapeDtypeStruct(tile.shape, tile.dtype),
        in_specs=[pl.BlockSpec(memory_space=pltpu.VMEM)],
        out_specs=pl.BlockSpec(memory_space=pltpu.VMEM),
        scratch_shapes=[
            pltpu.VMEM((devices,) + tile.shape, tile.dtype),
            pltpu.SemaphoreType.DMA((devices - 1,)),
            pltpu.SemaphoreType.DMA((devices - 1,)),
        ],
        compiler_params=pltpu.CompilerParams(collective_id=2, has_side_effects=True),
        name="total_over_devices",
    )(tile)


def ring_device(shift, inner):
    wide = lax.axis_size("wide")
    return (lax.rem(lax.axis_index("wide") + shift * inner + wide, wide), lax.axis_index("narrow"))


def entry_barrier(steps, inner, narrow):
    barrier = pltpu.get_barrier_semaphore()
    group = inner * narrow

    def greet(offset, carry):
        _, _, device = plane_peer(offset, inner, narrow)
        pl.semaphore_signal(barrier, inc=1, device_id=device, device_id_type=MESH)
        return carry

    lax.fori_loop(1, group, greet, 0)
    if steps > 1:
        for shift in (1, -1):
            pl.semaphore_signal(
                barrier, inc=1, device_id=ring_device(shift, inner), device_id_type=MESH
            )
    pl.semaphore_wait(barrier, group - 1 + (2 if steps > 1 else 0))


def gather_kernel(steps, inner, narrow, row_cap, col_cap, rows_ref, cols_ref, dens_ref, *rest):
    outs, rest = rest[:steps], rest[steps:]
    raws, rest = rest[:steps], rest[steps:]
    chosen, send_sem, recv_sem, ring_send, ring_recv, own_sem, load_sem = rest
    group = inner * narrow
    ring_me = lax.axis_index("wide") // inner
    mine, _, _ = plane_peer(0, inner, narrow)
    col_blocks = dens_ref.shape[1] // BLK
    held = raws[0].shape[0]
    half = held // 2

    def load_copy(place):
        row, col = place // col_blocks, place % col_blocks
        return pltpu.make_async_copy(
            dens_ref.at[
                pl.ds(pl.multiple_of(row * BLK, BLK), BLK),
                pl.ds(pl.multiple_of(col * BLK, BLK), BLK),
            ],
            raws[0].at[place],
            load_sem.at[place],
        )

    def load(place, carry):
        load_copy(place).start()
        return carry

    def loaded(place, carry):
        load_copy(place).wait()
        return carry

    def pick(step):
        ring = lax.rem(ring_me - step + steps, steps)

        def body(offset, carry):
            _, other, _ = plane_peer(offset, inner, narrow)
            for rr in range(row_cap):
                row = rows_ref[other, ring * row_cap + rr] * col_blocks
                for cr in range(col_cap):
                    place = row + cols_ref[other, cr]
                    chosen[step, offset, rr * col_cap + cr] = raws[step][place]
            return carry

        lax.fori_loop(0, group, body, 0)

    def block_copy(step, offset):
        _, _, device = plane_peer(offset, inner, narrow)
        return pltpu.make_async_remote_copy(
            src_ref=chosen.at[step, offset],
            dst_ref=outs[step].at[mine],
            send_sem=send_sem.at[step, offset - 1],
            recv_sem=recv_sem.at[step, offset - 1],
            device_id=device,
            device_id_type=MESH,
        )

    def ring_copy(step, piece):
        span = pl.ds(piece * half, half)
        return pltpu.make_async_remote_copy(
            src_ref=raws[step].at[span],
            dst_ref=raws[step + 1].at[span],
            send_sem=ring_send.at[step, piece],
            recv_sem=ring_recv.at[step, piece],
            device_id=ring_device(1, inner),
            device_id_type=MESH,
        )

    def own_copy(step):
        return pltpu.make_async_copy(chosen.at[step, 0], outs[step].at[mine], own_sem.at[step])

    for step in range(steps):
        if step == 0:
            lax.fori_loop(0, held, load, 0)
            lax.fori_loop(0, held, loaded, 0)
            pick(0)
            entry_barrier(steps, inner, narrow)
        for piece in range(2):
            if step > 0:
                ring_copy(step - 1, piece).wait_recv()
            if step < steps - 1:
                ring_copy(step, piece).start()
        if step > 0:
            pick(step)

        def send(offset, carry, step=step):
            block_copy(step, offset).start()
            return carry

        lax.fori_loop(1, group, send, 0)
        own_copy(step).start()
    for step in range(steps):

        def finish(offset, carry, step=step):
            block_copy(step, offset).wait()
            return carry

        lax.fori_loop(1, group, finish, 0)
        own_copy(step).wait()
        if step < steps - 1:
            for piece in range(2):
                ring_copy(step, piece).wait_send()


def gather_blocks(dens, rows, cols, steps, inner, narrow, row_cap, col_cap):
    group = inner * narrow
    cap = row_cap * col_cap
    ring_sems = max(1, steps - 1)
    held = dens.shape[0] // BLK * (dens.shape[1] // BLK)
    return pl.pallas_call(
        functools.partial(gather_kernel, steps, inner, narrow, row_cap, col_cap),
        out_shape=[jax.ShapeDtypeStruct((group, cap, BLK, BLK), dens.dtype)] * steps,
        in_specs=[
            pl.BlockSpec(memory_space=pltpu.SMEM),
            pl.BlockSpec(memory_space=pltpu.SMEM),
            pl.BlockSpec(memory_space=pl.ANY),
        ],
        out_specs=[pl.BlockSpec(memory_space=pl.ANY)] * steps,
        scratch_shapes=[pltpu.VMEM((held, BLK, BLK), dens.dtype)] * steps
        + [
            pltpu.VMEM((steps, group, cap, BLK, BLK), dens.dtype),
            pltpu.SemaphoreType.DMA((steps, group - 1)),
            pltpu.SemaphoreType.DMA((steps, group - 1)),
            pltpu.SemaphoreType.DMA((ring_sems, 2)),
            pltpu.SemaphoreType.DMA((ring_sems, 2)),
            pltpu.SemaphoreType.DMA((steps,)),
            pltpu.SemaphoreType.DMA((held,)),
        ],
        compiler_params=pltpu.CompilerParams(
            collective_id=1, has_side_effects=True, vmem_limit_bytes=VMEM_BYTES
        ),
        name="gather_blocks",
    )(rows, cols, dens)


def return_kernel(steps, inner, narrow, cap, rows_ref, cols_ref, *rest):
    parts, rest = rest[:steps], rest[steps:]
    out_ref, rest = rest[0], rest[1:]
    gots, rest = rest[:steps], rest[steps:]
    runs, rest = rest[: steps - 1], rest[steps - 1 :]
    prevs, rest = (None,) + rest[: steps - 1], rest[steps - 1 :]
    send_sem, recv_sem, ring_send, ring_recv, own_sem = rest
    group = inner * narrow
    ring_me = lax.axis_index("wide") // inner
    mine, _, _ = plane_peer(0, inner, narrow)
    row_blocks = out_ref.shape[0] // BLK
    col_blocks = out_ref.shape[1] // BLK
    empty = group * cap

    def block_copy(step, offset):
        _, other, device = plane_peer(offset, inner, narrow)
        return pltpu.make_async_remote_copy(
            src_ref=parts[step].at[pl.ds(other * cap, cap)],
            dst_ref=gots[step].at[pl.ds(mine * cap, cap)],
            send_sem=send_sem.at[step, offset - 1],
            recv_sem=recv_sem.at[step, offset - 1],
            device_id=device,
            device_id_type=MESH,
        )

    def own_copy(step):
        span = pl.ds(mine * cap, cap)
        return pltpu.make_async_copy(parts[step].at[span], gots[step].at[span], own_sem.at[step])

    def ring_copy(step, piece):
        span = pl.ds(piece * BLK, BLK)
        return pltpu.make_async_remote_copy(
            src_ref=runs[step].at[span],
            dst_ref=prevs[step + 1].at[span],
            send_sem=ring_send.at[step, piece],
            recv_sem=ring_recv.at[step, piece],
            device_id=ring_device(1, inner),
            device_id_type=MESH,
        )

    def start_step(step):
        own_copy(step).start()

        def send(offset, carry):
            block_copy(step, offset).start()
            return carry

        lax.fori_loop(1, group, send, 0)

    for step in range(steps):
        gots[step][empty] = jnp.zeros((BLK, BLK), gots[step].dtype)
    entry_barrier(steps, inner, narrow)
    for step in range(min(2, steps)):
        start_step(step)
    for step in range(steps):
        last = step == steps - 1
        ring = lax.rem(ring_me - 1 - step + 2 * steps, steps)

        def arrive(offset, carry, step=step):
            block_copy(step, offset).wait_recv()
            return carry

        lax.fori_loop(1, group, arrive, 0)
        own_copy(step).wait()
        if step + 2 < steps:
            start_step(step + 2)

        def add_row(piece, carry, step=step, last=last, ring=ring):
            if step > 0:
                ring_copy(step - 1, piece).wait_recv()
            span = pl.ds(pl.multiple_of(piece * BLK, BLK), BLK)
            bases = [
                rows_ref[source, ring * row_blocks + piece] + source * cap
                for source in range(group)
            ]

            def add_block(block, inner_carry):
                across = pl.ds(pl.multiple_of(block * BLK, BLK), BLK)
                if step > 0:
                    total = prevs[step][span, across].astype(jnp.float32)
                else:
                    total = jnp.zeros((BLK, BLK), jnp.float32)
                for source in range(group):
                    place = jnp.minimum(bases[source] + cols_ref[source, block], empty)
                    total += gots[step][place].astype(jnp.float32)
                if last:
                    out_ref[span, across] = total
                else:
                    runs[step][span, across] = total.astype(runs[step].dtype)
                return inner_carry

            lax.fori_loop(0, col_blocks, add_block, 0)
            if not last:

                @pl.when(piece > 0)
                def _():
                    ring_copy(step, piece - 1).start()

            return carry

        lax.fori_loop(0, row_blocks, add_row, 0)
        if not last:
            ring_copy(step, row_blocks - 1).start()
    for step in range(steps):

        def finish(offset, carry, step=step):
            block_copy(step, offset).wait_send()
            return carry

        lax.fori_loop(1, group, finish, 0)
        if step < steps - 1:

            def left(piece, carry, step=step):
                ring_copy(step, piece).wait_send()
                return carry

            lax.fori_loop(0, row_blocks, left, 0)


def return_blocks(parts, rows, cols, shape, steps, inner, narrow, cap):
    group = inner * narrow
    ring_sems = max(1, steps - 1)
    row_blocks = shape[0] // BLK
    dtype = parts[0].dtype
    return pl.pallas_call(
        functools.partial(return_kernel, steps, inner, narrow, cap),
        out_shape=jax.ShapeDtypeStruct(shape, jnp.float32),
        in_specs=[pl.BlockSpec(memory_space=pltpu.SMEM)] * 2
        + [pl.BlockSpec(memory_space=pl.ANY)] * steps,
        out_specs=pl.BlockSpec(memory_space=pltpu.VMEM),
        scratch_shapes=[pltpu.VMEM((group * cap + 1, BLK, BLK), dtype)] * steps
        + [pltpu.VMEM(shape, dtype)] * (2 * (steps - 1))
        + [
            pltpu.SemaphoreType.DMA((steps, group - 1)),
            pltpu.SemaphoreType.DMA((steps, group - 1)),
            pltpu.SemaphoreType.DMA((ring_sems, row_blocks)),
            pltpu.SemaphoreType.DMA((ring_sems, row_blocks)),
            pltpu.SemaphoreType.DMA((steps,)),
        ],
        compiler_params=pltpu.CompilerParams(
            collective_id=3, has_side_effects=True, vmem_limit_bytes=VMEM_BYTES
        ),
        name="return_blocks",
    )(rows, cols, *parts)


def live_row(weights_ref, counts_ref, batch):
    points = weights_ref.shape[1]
    point = lax.broadcasted_iota(jnp.int32, (1, points), 1)
    return jnp.where(
        point < counts_ref[batch], weights_ref[pl.ds(batch, 1), :], jnp.float32(0.0)
    )


def density_kernel(
    steps, list_len, lists_ref, row_ref, col_ref, counts_ref, orb_ref, harm_ref, weights_ref, *rest
):
    chunks = rest[:steps]
    rho_ref, moment_ref, held, matrix, sems = rest[steps:]
    batch = pl.program_id(0)
    per_chunk = held.shape[0] // steps

    @pl.when(batch == 0)
    def _():
        copies = [
            pltpu.make_async_copy(
                chunks[k], held.at[pl.ds(k * per_chunk, per_chunk)], sems.at[k]
            )
            for k in range(steps)
        ]
        for copy in copies:
            copy.start()
        moment_ref[...] = jnp.zeros_like(moment_ref)
        for copy in copies:
            copy.wait()

    places = [lists_ref[batch, k] for k in range(list_len)]
    cols = [col_ref[place] for place in places]
    for k in range(list_len):
        row = row_ref[places[k]]
        for k2 in range(list_len):
            matrix[k * BLK : (k + 1) * BLK, k2 * BLK : (k2 + 1) * BLK] = held[row + cols[k2]]
    orbs = orb_ref[0]
    rows_each = 2 * BLK
    total = jnp.zeros((1, orbs.shape[1]), jnp.float32)
    for top in range(0, list_len * BLK, rows_each):
        product = jnp.dot(
            matrix[top : top + rows_each, :], orbs, preferred_element_type=jnp.float32
        )
        part = product * orb_ref[0, top : top + rows_each, :].astype(jnp.float32)
        total += jnp.sum(part, axis=0, keepdims=True)
    rho_ref[pl.ds(batch, 1), :] = total
    live = live_row(weights_ref, counts_ref, batch) * total
    moment_ref[...] += harm_ref[0].astype(jnp.float32) * live


def density_points(lists, rows, cols, counts, orbitals, harmonics, weights, chunks):
    batches, height, points = orbitals.shape
    list_len = lists.shape[1]
    components = harmonics.shape[1]
    steps = len(chunks)
    blocks = [chunk.reshape(-1, BLK, BLK) for chunk in chunks]
    held = steps * blocks[0].shape[0]
    full = lambda shape: pl.BlockSpec(shape, lambda g, *_: (0, 0))
    return pl.pallas_call(
        functools.partial(density_kernel, steps, list_len),
        out_shape=[
            jax.ShapeDtypeStruct((batches, points), jnp.float32),
            jax.ShapeDtypeStruct((components, points), jnp.float32),
        ],
        grid_spec=pltpu.PrefetchScalarGridSpec(
            num_scalar_prefetch=4,
            grid=(batches,),
            in_specs=[
                pl.BlockSpec((1, height, points), lambda g, *_: (g, 0, 0)),
                pl.BlockSpec((1, components, points), lambda g, *_: (g, 0, 0)),
                full((batches, points)),
            ]
            + [pl.BlockSpec(memory_space=pl.ANY)] * steps,
            out_specs=[full((batches, points)), full((components, points))],
            scratch_shapes=[
                pltpu.VMEM((held, BLK, BLK), jnp.bfloat16),
                pltpu.VMEM((height, height), jnp.bfloat16),
                pltpu.SemaphoreType.DMA((steps,)),
            ],
        ),
        compiler_params=pltpu.CompilerParams(vmem_limit_bytes=VMEM_BYTES),
        name="density_points",
    )(lists, rows, cols, counts, orbitals, harmonics, weights, *blocks)


def integral_kernel(
    steps,
    list_len,
    far_scale,
    lists_ref,
    row_ref,
    col_ref,
    counts_ref,
    orb_ref,
    harm_ref,
    weights_ref,
    rho_ref,
    moment_ref,
    *rest,
):
    outs = rest[:steps]
    acc, stage, sems = rest[steps:]
    batch = pl.program_id(0)
    per_chunk = acc.shape[0] // steps

    @pl.when(batch == 0)
    def _():
        @pl.loop(0, acc.shape[0])
        def _(place):
            acc[place] = jnp.zeros(acc.shape[1:], jnp.float32)

    rho = rho_ref[pl.ds(batch, 1), :]
    far = FAR_COEFF * jnp.sum(
        moment_ref[...] * harm_ref[0].astype(jnp.float32), axis=0, keepdims=True
    )
    sixth = jnp.exp(jnp.log(1.0 + rho * rho) * (1.0 / 6.0))
    potential = 0.5 * rho - sixth + far / far_scale
    factor = live_row(weights_ref, counts_ref, batch) * potential
    orbs = orb_ref[0]
    scaled = (orbs.astype(jnp.float32) * factor).astype(jnp.bfloat16)
    places = [lists_ref[batch, k] for k in range(list_len)]
    rows = [row_ref[place] for place in places]
    cols = [col_ref[place] for place in places]
    for pair in range(0, list_len, 2):
        right = orb_ref[0, pair * BLK : (pair + 2) * BLK, :]
        term = lax.dot_general(
            scaled, right, (((1,), (1,)), ((), ())), preferred_element_type=jnp.float32
        )
        for k in range(list_len):
            for k2 in range(2):
                acc[rows[k] + cols[pair + k2]] += term[
                    k * BLK : (k + 1) * BLK, k2 * BLK : (k2 + 1) * BLK
                ]

    @pl.when(batch == pl.num_programs(0) - 1)
    def _():
        copies = []
        for k in range(steps):
            if k >= 2:
                copies[k - 2].wait()

            @pl.loop(0, per_chunk)
            def _(place, k=k):
                stage[k % 2, place] = acc[k * per_chunk + place].astype(jnp.bfloat16)

            copy = pltpu.make_async_copy(stage.at[k % 2], outs[k], sems.at[k])
            copy.start()
            copies.append(copy)
        for copy in copies[-2:]:
            copy.wait()


def integrals(lists, rows, cols, counts, orbitals, harmonics, weights, rho, moments, steps, held, far_scale):
    batches, height, points = orbitals.shape
    list_len = lists.shape[1]
    components = harmonics.shape[1]
    per_chunk = held // steps
    full = lambda shape: pl.BlockSpec(shape, lambda g, *_: (0, 0))
    return pl.pallas_call(
        functools.partial(integral_kernel, steps, list_len, far_scale),
        out_shape=[jax.ShapeDtypeStruct((per_chunk, BLK, BLK), jnp.bfloat16)] * steps,
        grid_spec=pltpu.PrefetchScalarGridSpec(
            num_scalar_prefetch=4,
            grid=(batches,),
            in_specs=[
                pl.BlockSpec((1, height, points), lambda g, *_: (g, 0, 0)),
                pl.BlockSpec((1, components, points), lambda g, *_: (g, 0, 0)),
                full((batches, points)),
                full((batches, points)),
                full((components, 1)),
            ],
            out_specs=[pl.BlockSpec(memory_space=pl.ANY)] * steps,
            scratch_shapes=[
                pltpu.VMEM((held, BLK, BLK), jnp.float32),
                pltpu.VMEM((2, per_chunk, BLK, BLK), jnp.bfloat16),
                pltpu.SemaphoreType.DMA((steps,)),
            ],
        ),
        compiler_params=pltpu.CompilerParams(vmem_limit_bytes=VMEM_BYTES),
        name="integrals",
    )(lists, rows, cols, counts, orbitals, harmonics, weights, rho, moments)


def rank_among(keys):
    count = keys.shape[0]
    order = jnp.arange(count)
    same = (keys[:, None] == keys[None, :]) & (order[None, :] < order[:, None])
    return jnp.sum(same.astype(jnp.int32), axis=1)


def spread(positions, values, size):
    hit = positions[None, :] == jnp.arange(size)[:, None]
    return jnp.sum(jnp.where(hit, values[None, :], 0), axis=1)


def per_device(
    region, density, block_slot, region_blocks, basis_lists, point_counts, orbitals, weights, harmonics
):
    wide = lax.axis_size("wide")
    narrow = lax.axis_size("narrow")
    devices = wide * narrow
    steps = math.gcd(wide, RING)
    inner = wide // steps
    group = inner * narrow
    row_cap = max(1, region // wide)
    col_cap = region // narrow
    cap = row_cap * col_cap
    wide_me = lax.axis_index("wide")
    narrow_me = lax.axis_index("narrow")
    ring_me = wide_me // inner
    inner_me = wide_me % inner

    known = block_slot.shape[0]
    hit = region_blocks[:, None] == jnp.arange(known)[None, :]
    slots = jnp.sum(jnp.where(hit, block_slot[None, :], 0), axis=1)
    row_owner, row_local = slots % wide, slots // wide
    col_owner, col_local = slots % narrow, slots // narrow
    row_rank, col_rank = rank_among(row_owner), rank_among(col_owner)
    row_table = spread(row_owner * row_cap + row_rank, row_local, LANES)
    col_table = spread(col_owner * col_cap + col_rank, col_local, LANES)
    far = 1 << 20
    row_blocks = density.shape[0] // BLK
    col_blocks = density.shape[1] // BLK
    row_back = far + spread(
        row_owner * row_blocks + row_local, row_rank * col_cap - far, LANES
    )
    col_back = far + spread(col_owner * col_blocks + col_local, col_rank - far, LANES)
    tile = jnp.stack([row_table, col_table, row_back, col_back] * 2)
    tables = share_tile(tile, inner, narrow)

    def rows_here(plane, each):
        used = tables[:, plane, : wide * each].reshape(group, steps, inner, each)
        one = lax.dynamic_index_in_dim(used, inner_me, axis=2, keepdims=False)
        return one.reshape(group, steps * each)

    def cols_here(plane, each):
        return lax.dynamic_slice_in_dim(tables[:, plane], narrow_me * each, each, axis=1)

    chunks = gather_blocks(
        density,
        rows_here(0, row_cap),
        cols_here(1, col_cap),
        steps,
        inner,
        narrow,
        row_cap,
        col_cap,
    )

    col_place = col_owner * cap + col_rank
    in_plane = row_owner % inner * (narrow * cap) + row_rank * col_cap
    owner_ring = row_owner // inner
    row_in = (ring_me - owner_ring + steps) % steps * (group * cap) + in_plane
    row_out = (ring_me - 1 - owner_ring + 2 * steps) % steps * (group * cap) + in_plane

    rho, moment_parts = density_points(
        basis_lists, row_in, col_place, point_counts, orbitals, harmonics, weights, chunks
    )
    components = harmonics.shape[1]
    local = jnp.sum(moment_parts, axis=1)
    tile = jnp.zeros((8, LANES), jnp.float32).at[0, :components].set(local)
    moments = total_over_devices(tile, devices, narrow)[0, :components].reshape(components, 1)

    total_points = orbitals.shape[0] * orbitals.shape[2] * devices
    parts = integrals(
        basis_lists,
        row_out,
        col_place,
        point_counts,
        orbitals,
        harmonics,
        weights,
        rho,
        moments,
        steps,
        steps * group * cap,
        math.sqrt(total_points * components),
    )
    return return_blocks(
        parts,
        rows_here(2, row_blocks),
        cols_here(3, col_blocks),
        density.shape,
        steps,
        inner,
        narrow,
        cap,
    )


def solution(mesh):
    devices = mesh.shape["wide"] * mesh.shape["narrow"]

    def whole(density, block_slot, region_blocks, *others):
        region = region_blocks.shape[0] // devices
        in_specs = (
            P("wide", "narrow"),
            P(),
            P(("wide", "narrow")),
            P(("wide", "narrow"), None),
            P(("wide", "narrow")),
            P(("wide", "narrow"), None, None),
            P(("wide", "narrow"), None),
            P(("wide", "narrow"), None, None),
        )
        mapped = jax.shard_map(
            functools.partial(per_device, region),
            mesh=mesh,
            in_specs=in_specs,
            out_specs=P("wide", "narrow"),
            check_vma=False,
        )
        return mapped(density, block_slot, region_blocks, *others)

    return whole
```

```python
import functools
import math

import jax
import jax.numpy as jnp
from jax import lax
from jax.experimental import pallas as pl
from jax.experimental.pallas import tpu as pltpu
from jax.sharding import PartitionSpec as P

BLK = 128
FAR_COEFF = 10.0
RING = 4
LANES = 128
MESH = pl.DeviceIdType.MESH
VMEM_BYTES = 58 * 1024 * 1024


def plane_peer(offset, inner, narrow):
    wide_me = lax.axis_index("wide")
    group = inner * narrow
    base = wide_me // inner * inner
    mine = wide_me % inner * narrow + lax.axis_index("narrow")
    other = lax.rem(mine + offset, group)
    return mine, other, (base + other // narrow, other % narrow)


def ring_device(shift, inner):
    wide = lax.axis_size("wide")
    return (lax.rem(lax.axis_index("wide") + shift * inner + wide, wide), lax.axis_index("narrow"))


def entry_barrier(steps, inner, narrow):
    barrier = pltpu.get_barrier_semaphore()
    group = inner * narrow

    def greet(offset, carry):
        _, _, device = plane_peer(offset, inner, narrow)
        pl.semaphore_signal(barrier, inc=1, device_id=device, device_id_type=MESH)
        return carry

    lax.fori_loop(1, group, greet, 0)
    if steps > 1:
        for shift in (1, -1):
            pl.semaphore_signal(
                barrier, inc=1, device_id=ring_device(shift, inner), device_id_type=MESH
            )
    pl.semaphore_wait(barrier, group - 1 + (2 if steps > 1 else 0))


def any_device(offset):
    narrow = lax.axis_size("narrow")
    devices = lax.axis_size("wide") * narrow
    mine = lax.axis_index("wide") * narrow + lax.axis_index("narrow")
    other = lax.rem(mine + offset, devices)
    return mine, (other // narrow, other % narrow)


def gather_kernel(
    steps,
    inner,
    narrow,
    row_cap,
    col_cap,
    lists_ref,
    row_ref,
    col_ref,
    counts_ref,
    tile_ref,
    weights_ref,
    dens_ref,
    orb_ref,
    harm_ref,
    tables_ref,
    rho_ref,
    total_ref,
    *rest,
):
    arrived, rest = rest[0], rest[1:]
    raws, rest = rest[:steps], rest[steps:]
    (
        chosen,
        table,
        orbs,
        harms,
        matrix,
        moment,
        share,
        shares,
        send_sem,
        recv_sem,
        ring_send,
        ring_recv,
        own_sem,
        load_sem,
        tile_send,
        tile_recv,
        local_sem,
        share_send,
        share_recv,
    ) = rest
    devices = lax.axis_size("wide") * narrow
    inner_me = lax.axis_index("wide") % inner
    narrow_me = lax.axis_index("narrow")
    cap = row_cap * col_cap
    group = inner * narrow
    ring_me = lax.axis_index("wide") // inner
    mine, _, _ = plane_peer(0, inner, narrow)
    col_blocks = dens_ref.shape[1] // BLK
    held = raws[0].shape[0]
    half = held // 2

    def load_copy(place):
        row, col = place // col_blocks, place % col_blocks
        return pltpu.make_async_copy(
            dens_ref.at[
                pl.ds(pl.multiple_of(row * BLK, BLK), BLK),
                pl.ds(pl.multiple_of(col * BLK, BLK), BLK),
            ],
            raws[0].at[place],
            load_sem.at[place],
        )

    def load(place, carry):
        load_copy(place).start()
        return carry

    def loaded(place, carry):
        load_copy(place).wait()
        return carry

    def pick(step):
        ring = lax.rem(ring_me - step + steps, steps)

        def body(offset, carry):
            _, other, _ = plane_peer(offset, inner, narrow)
            for rr in range(row_cap):
                row = table[other, 0, (ring * inner + inner_me) * row_cap + rr] * col_blocks
                for cr in range(col_cap):
                    place = row + table[other, 1, narrow_me * col_cap + cr]
                    chosen[step, offset, rr * col_cap + cr] = raws[step][place]
            return carry

        lax.fori_loop(0, group, body, 0)

    def block_copy(step, offset):
        _, _, device = plane_peer(offset, inner, narrow)
        return pltpu.make_async_remote_copy(
            src_ref=chosen.at[step, offset],
            dst_ref=arrived.at[pl.ds((step * group + mine) * cap, cap)],
            send_sem=send_sem.at[step, offset - 1],
            recv_sem=recv_sem.at[step, offset - 1],
            device_id=device,
            device_id_type=MESH,
        )

    def ring_copy(step, piece):
        span = pl.ds(piece * half, half)
        return pltpu.make_async_remote_copy(
            src_ref=raws[step].at[span],
            dst_ref=raws[step + 1].at[span],
            send_sem=ring_send.at[step, piece],
            recv_sem=ring_recv.at[step, piece],
            device_id=ring_device(1, inner),
            device_id_type=MESH,
        )

    def own_copy(step):
        return pltpu.make_async_copy(
            chosen.at[step, 0],
            arrived.at[pl.ds((step * group + mine) * cap, cap)],
            own_sem.at[step],
        )

    def tile_copy(offset):
        _, _, device = plane_peer(offset, inner, narrow)
        return pltpu.make_async_remote_copy(
            src_ref=tile_ref,
            dst_ref=tables_ref.at[mine],
            send_sem=tile_send.at[offset - 1],
            recv_sem=tile_recv.at[offset - 1],
            device_id=device,
            device_id_type=MESH,
        )

    def share_copy(offset):
        whose, device = any_device(offset)
        return pltpu.make_async_remote_copy(
            src_ref=share,
            dst_ref=shares.at[whose],
            send_sem=share_send.at[offset - 1],
            recv_sem=share_recv.at[offset - 1],
            device_id=device,
            device_id_type=MESH,
        )

    def over(count, make, act):
        def body(offset, carry):
            act(make(offset))
            return carry

        lax.fori_loop(1, count, body, 0)

    start = lambda copy: copy.start()
    wait = lambda copy: copy.wait()

    load_orbs = pltpu.make_async_copy(orb_ref, orbs, local_sem.at[0])
    load_harms = pltpu.make_async_copy(harm_ref, harms, local_sem.at[1])
    for step in range(steps):
        if step == 0:
            tables_ref[mine] = tile_ref[...]
            lax.fori_loop(0, held, load, 0)
            barrier = pltpu.get_barrier_semaphore()

            def greet(offset, carry):
                _, device = any_device(offset)
                pl.semaphore_signal(barrier, inc=1, device_id=device, device_id_type=MESH)
                return carry

            lax.fori_loop(1, devices, greet, 0)
            load_orbs.start()
            load_harms.start()
            lax.fori_loop(0, held, loaded, 0)
            pl.semaphore_wait(barrier, devices - 1)
            over(group, tile_copy, start)
        for piece in range(2):
            if step > 0:
                ring_copy(step - 1, piece).wait_recv()
            if step < steps - 1:
                ring_copy(step, piece).start()
        if step == 0:
            over(group, tile_copy, wait)
            to_table = pltpu.make_async_copy(tables_ref, table, local_sem.at[2])
            to_table.start()
            to_table.wait()
        pick(step)

        def send(offset, carry, step=step):
            block_copy(step, offset).start()
            return carry

        lax.fori_loop(1, group, send, 0)
        own_copy(step).start()
    for step in range(steps):

        def finish(offset, carry, step=step):
            block_copy(step, offset).wait()
            return carry

        lax.fori_loop(1, group, finish, 0)
        own_copy(step).wait()
        if step < steps - 1:
            for piece in range(2):
                ring_copy(step, piece).wait_send()
    load_orbs.wait()
    load_harms.wait()

    list_len = lists_ref.shape[1]
    height, points = orbs.shape[1:]
    each = 2 * BLK
    moment[...] = jnp.zeros_like(moment)

    def add_batch(batch, carry):
        places = [lists_ref[batch, k] for k in range(list_len)]
        cols = [col_ref[place] for place in places]
        for k in range(list_len):
            row = row_ref[places[k]]
            for k2 in range(list_len):
                spot = row + cols[k2]
                matrix[k * BLK : (k + 1) * BLK, k2 * BLK : (k2 + 1) * BLK] = arrived[spot]
        total = jnp.zeros((1, points), jnp.float32)
        for top in range(0, height, each):
            product = jnp.dot(
                matrix[top : top + each, :], orbs[batch], preferred_element_type=jnp.float32
            )
            part = product * orbs[batch, top : top + each, :].astype(jnp.float32)
            total += jnp.sum(part, axis=0, keepdims=True)
        rho_ref[pl.ds(batch, 1), :] = total
        live = live_row(weights_ref, counts_ref, batch) * total
        moment[...] += harms[batch].astype(jnp.float32) * live
        return carry

    lax.fori_loop(0, orbs.shape[0], add_batch, 0)
    components = moment.shape[0]
    diagonal = lax.broadcasted_iota(jnp.int32, (components, LANES), 0) == lax.broadcasted_iota(
        jnp.int32, (components, LANES), 1
    )
    summed = jnp.sum(moment[...], axis=1, keepdims=True)
    line = jnp.sum(jnp.where(diagonal, summed, 0.0), axis=0, keepdims=True)
    share[...] = jnp.broadcast_to(line, share.shape)
    whose, _ = any_device(0)
    shares[whose] = jnp.broadcast_to(line, share.shape)
    over(devices, share_copy, start)
    over(devices, share_copy, wait)
    line = jnp.sum(shares[...], axis=0)[0:1]
    total_ref[...] = jnp.sum(jnp.where(diagonal, line, 0.0), axis=1, keepdims=True)


def gather_density(
    lists, rows, cols, counts, tile, weights, dens, orbitals, harmonics, steps, inner, narrow, caps
):
    row_cap, col_cap = caps
    group = inner * narrow
    cap = row_cap * col_cap
    devices = steps * group
    ring_sems = max(1, steps - 1)
    held = dens.shape[0] // BLK * (dens.shape[1] // BLK)
    batches, height, points = orbitals.shape
    components = harmonics.shape[1]
    vmem = pl.BlockSpec(memory_space=pltpu.VMEM)
    smem = pl.BlockSpec(memory_space=pltpu.SMEM)
    anywhere = pl.BlockSpec(memory_space=pl.ANY)
    return pl.pallas_call(
        functools.partial(gather_kernel, steps, inner, narrow, row_cap, col_cap),
        out_shape=[
            jax.ShapeDtypeStruct((group,) + tile.shape, tile.dtype),
            jax.ShapeDtypeStruct((batches, points), jnp.float32),
            jax.ShapeDtypeStruct((components, 1), jnp.float32),
        ],
        in_specs=[smem] * 4 + [vmem] * 2 + [anywhere] * 3,
        out_specs=[vmem] * 3,
        scratch_shapes=[pltpu.VMEM((steps * group * cap, BLK, BLK), dens.dtype)]
        + [pltpu.VMEM((held, BLK, BLK), dens.dtype)] * steps
        + [
            pltpu.VMEM((steps, group, cap, BLK, BLK), dens.dtype),
            pltpu.SMEM((group,) + tile.shape, tile.dtype),
            pltpu.VMEM(orbitals.shape, orbitals.dtype),
            pltpu.VMEM(harmonics.shape, harmonics.dtype),
            pltpu.VMEM((height, height), dens.dtype),
            pltpu.VMEM((components, points), jnp.float32),
            pltpu.VMEM((8, LANES), jnp.float32),
            pltpu.VMEM((devices, 8, LANES), jnp.float32),
            pltpu.SemaphoreType.DMA((steps, group - 1)),
            pltpu.SemaphoreType.DMA((steps, group - 1)),
            pltpu.SemaphoreType.DMA((ring_sems, 2)),
            pltpu.SemaphoreType.DMA((ring_sems, 2)),
            pltpu.SemaphoreType.DMA((steps,)),
            pltpu.SemaphoreType.DMA((held,)),
            pltpu.SemaphoreType.DMA((group - 1,)),
            pltpu.SemaphoreType.DMA((group - 1,)),
            pltpu.SemaphoreType.DMA((3,)),
            pltpu.SemaphoreType.DMA((devices - 1,)),
            pltpu.SemaphoreType.DMA((devices - 1,)),
        ],
        compiler_params=pltpu.CompilerParams(
            collective_id=1, has_side_effects=True, vmem_limit_bytes=63 * 1024 * 1024
        ),
        name="gather_density",
    )(lists, rows, cols, counts, tile, weights, dens, orbitals, harmonics)


def return_kernel(steps, inner, narrow, cap, table_ref, *rest):
    parts, rest = rest[:steps], rest[steps:]
    out_ref, rest = rest[0], rest[1:]
    gots, rest = rest[:steps], rest[steps:]
    runs, rest = rest[: steps - 1], rest[steps - 1 :]
    prevs, rest = (None,) + rest[: steps - 1], rest[steps - 1 :]
    send_sem, recv_sem, ring_send, ring_recv, own_sem = rest
    group = inner * narrow
    ring_me = lax.axis_index("wide") // inner
    mine, _, _ = plane_peer(0, inner, narrow)
    row_blocks = out_ref.shape[0] // BLK
    col_blocks = out_ref.shape[1] // BLK
    empty = group * cap
    inner_me = lax.axis_index("wide") % inner
    narrow_me = lax.axis_index("narrow")

    def block_copy(step, offset):
        _, other, device = plane_peer(offset, inner, narrow)
        return pltpu.make_async_remote_copy(
            src_ref=parts[step].at[pl.ds(other * cap, cap)],
            dst_ref=gots[step].at[pl.ds(mine * cap, cap)],
            send_sem=send_sem.at[step, offset - 1],
            recv_sem=recv_sem.at[step, offset - 1],
            device_id=device,
            device_id_type=MESH,
        )

    def own_copy(step):
        span = pl.ds(mine * cap, cap)
        return pltpu.make_async_copy(parts[step].at[span], gots[step].at[span], own_sem.at[step])

    def ring_copy(step, piece):
        span = pl.ds(piece * BLK, BLK)
        return pltpu.make_async_remote_copy(
            src_ref=runs[step].at[span],
            dst_ref=prevs[step + 1].at[span],
            send_sem=ring_send.at[step, piece],
            recv_sem=ring_recv.at[step, piece],
            device_id=ring_device(1, inner),
            device_id_type=MESH,
        )

    def start_step(step):
        own_copy(step).start()

        def send(offset, carry):
            block_copy(step, offset).start()
            return carry

        lax.fori_loop(1, group, send, 0)

    for step in range(steps):
        gots[step][empty] = jnp.zeros((BLK, BLK), gots[step].dtype)
    entry_barrier(steps, inner, narrow)
    for step in range(min(2, steps)):
        start_step(step)
    for step in range(steps):
        last = step == steps - 1
        ring = lax.rem(ring_me - 1 - step + 2 * steps, steps)

        def arrive(offset, carry, step=step):
            block_copy(step, offset).wait_recv()
            return carry

        lax.fori_loop(1, group, arrive, 0)
        own_copy(step).wait()
        if step + 2 < steps:
            start_step(step + 2)

        def add_row(piece, carry, step=step, last=last, ring=ring):
            if step > 0:
                ring_copy(step - 1, piece).wait_recv()
            span = pl.ds(pl.multiple_of(piece * BLK, BLK), BLK)
            bases = [
                table_ref[source, 2, (ring * inner + inner_me) * row_blocks + piece] + source * cap
                for source in range(group)
            ]

            def add_block(block, inner_carry):
                across = pl.ds(pl.multiple_of(block * BLK, BLK), BLK)
                if step > 0:
                    total = prevs[step][span, across].astype(jnp.float32)
                else:
                    total = jnp.zeros((BLK, BLK), jnp.float32)
                for source in range(group):
                    col = table_ref[source, 3, narrow_me * col_blocks + block]
                    place = jnp.minimum(bases[source] + col, empty)
                    total += gots[step][place].astype(jnp.float32)
                if last:
                    out_ref[span, across] = total
                else:
                    runs[step][span, across] = total.astype(runs[step].dtype)
                return inner_carry

            lax.fori_loop(0, col_blocks, add_block, 0)
            if not last:

                @pl.when(piece > 0)
                def _():
                    ring_copy(step, piece - 1).start()

            return carry

        lax.fori_loop(0, row_blocks, add_row, 0)
        if not last:
            ring_copy(step, row_blocks - 1).start()
    for step in range(steps):

        def finish(offset, carry, step=step):
            block_copy(step, offset).wait_send()
            return carry

        lax.fori_loop(1, group, finish, 0)
        if step < steps - 1:

            def left(piece, carry, step=step):
                ring_copy(step, piece).wait_send()
                return carry

            lax.fori_loop(0, row_blocks, left, 0)


def return_blocks(parts, tables, shape, steps, inner, narrow, cap):
    group = inner * narrow
    ring_sems = max(1, steps - 1)
    row_blocks = shape[0] // BLK
    dtype = parts[0].dtype
    return pl.pallas_call(
        functools.partial(return_kernel, steps, inner, narrow, cap),
        out_shape=jax.ShapeDtypeStruct(shape, jnp.float32),
        in_specs=[pl.BlockSpec(memory_space=pltpu.SMEM)]
        + [pl.BlockSpec(memory_space=pl.ANY)] * steps,
        out_specs=pl.BlockSpec(memory_space=pltpu.VMEM),
        scratch_shapes=[pltpu.VMEM((group * cap + 1, BLK, BLK), dtype)] * steps
        + [pltpu.VMEM(shape, dtype)] * (2 * (steps - 1))
        + [
            pltpu.SemaphoreType.DMA((steps, group - 1)),
            pltpu.SemaphoreType.DMA((steps, group - 1)),
            pltpu.SemaphoreType.DMA((ring_sems, row_blocks)),
            pltpu.SemaphoreType.DMA((ring_sems, row_blocks)),
            pltpu.SemaphoreType.DMA((steps,)),
        ],
        compiler_params=pltpu.CompilerParams(
            collective_id=3, has_side_effects=True, vmem_limit_bytes=VMEM_BYTES
        ),
        name="return_blocks",
    )(tables, *parts)


def live_row(weights_ref, counts_ref, batch):
    points = weights_ref.shape[1]
    point = lax.broadcasted_iota(jnp.int32, (1, points), 1)
    return jnp.where(
        point < counts_ref[batch], weights_ref[pl.ds(batch, 1), :], jnp.float32(0.0)
    )


def integral_kernel(
    steps,
    list_len,
    far_scale,
    lists_ref,
    row_ref,
    col_ref,
    counts_ref,
    orb_ref,
    harm_ref,
    weights_ref,
    rho_ref,
    moment_ref,
    *rest,
):
    outs = rest[:steps]
    acc, stage, sems = rest[steps:]
    batch = pl.program_id(0)
    per_chunk = acc.shape[0] // steps

    @pl.when(batch == 0)
    def _():
        @pl.loop(0, acc.shape[0])
        def _(place):
            acc[place] = jnp.zeros(acc.shape[1:], jnp.float32)

    rho = rho_ref[pl.ds(batch, 1), :]
    far = FAR_COEFF * jnp.sum(
        moment_ref[...] * harm_ref[0].astype(jnp.float32), axis=0, keepdims=True
    )
    sixth = jnp.exp(jnp.log(1.0 + rho * rho) * (1.0 / 6.0))
    potential = 0.5 * rho - sixth + far / far_scale
    factor = live_row(weights_ref, counts_ref, batch) * potential
    orbs = orb_ref[0]
    scaled = (orbs.astype(jnp.float32) * factor).astype(jnp.bfloat16)
    places = [lists_ref[batch, k] for k in range(list_len)]
    rows = [row_ref[place] for place in places]
    cols = [col_ref[place] for place in places]
    for pair in range(0, list_len, 2):
        right = orb_ref[0, pair * BLK : (pair + 2) * BLK, :]
        term = lax.dot_general(
            scaled, right, (((1,), (1,)), ((), ())), preferred_element_type=jnp.float32
        )
        for k in range(list_len):
            for k2 in range(2):
                acc[rows[k] + cols[pair + k2]] += term[
                    k * BLK : (k + 1) * BLK, k2 * BLK : (k2 + 1) * BLK
                ]

    @pl.when(batch == pl.num_programs(0) - 1)
    def _():
        copies = []
        for k in range(steps):
            if k >= 2:
                copies[k - 2].wait()

            @pl.loop(0, per_chunk)
            def _(place, k=k):
                stage[k % 2, place] = acc[k * per_chunk + place].astype(jnp.bfloat16)

            copy = pltpu.make_async_copy(stage.at[k % 2], outs[k], sems.at[k])
            copy.start()
            copies.append(copy)
        for copy in copies[-2:]:
            copy.wait()


def integrals(lists, rows, cols, counts, orbitals, harmonics, weights, rho, moments, steps, held, far_scale):
    batches, height, points = orbitals.shape
    list_len = lists.shape[1]
    components = harmonics.shape[1]
    per_chunk = held // steps
    full = lambda shape: pl.BlockSpec(shape, lambda g, *_: (0, 0))
    return pl.pallas_call(
        functools.partial(integral_kernel, steps, list_len, far_scale),
        out_shape=[jax.ShapeDtypeStruct((per_chunk, BLK, BLK), jnp.bfloat16)] * steps,
        grid_spec=pltpu.PrefetchScalarGridSpec(
            num_scalar_prefetch=4,
            grid=(batches,),
            in_specs=[
                pl.BlockSpec((1, height, points), lambda g, *_: (g, 0, 0)),
                pl.BlockSpec((1, components, points), lambda g, *_: (g, 0, 0)),
                full((batches, points)),
                full((batches, points)),
                full((components, 1)),
            ],
            out_specs=[pl.BlockSpec(memory_space=pl.ANY)] * steps,
            scratch_shapes=[
                pltpu.VMEM((held, BLK, BLK), jnp.float32),
                pltpu.VMEM((2, per_chunk, BLK, BLK), jnp.bfloat16),
                pltpu.SemaphoreType.DMA((steps,)),
            ],
        ),
        compiler_params=pltpu.CompilerParams(vmem_limit_bytes=VMEM_BYTES),
        name="integrals",
    )(lists, rows, cols, counts, orbitals, harmonics, weights, rho, moments)


def rank_among(keys):
    count = keys.shape[0]
    order = jnp.arange(count)
    same = (keys[:, None] == keys[None, :]) & (order[None, :] < order[:, None])
    return jnp.sum(same.astype(jnp.int32), axis=1)


def spread(positions, values, size):
    hit = positions[None, :] == jnp.arange(size)[:, None]
    return jnp.sum(jnp.where(hit, values[None, :], 0), axis=1)


def per_device(
    region, density, block_slot, region_blocks, basis_lists, point_counts, orbitals, weights, harmonics
):
    wide = lax.axis_size("wide")
    narrow = lax.axis_size("narrow")
    devices = wide * narrow
    steps = math.gcd(wide, RING)
    inner = wide // steps
    group = inner * narrow
    row_cap = max(1, region // wide)
    col_cap = region // narrow
    cap = row_cap * col_cap
    wide_me = lax.axis_index("wide")
    ring_me = wide_me // inner

    known = block_slot.shape[0]
    hit = region_blocks[:, None] == jnp.arange(known)[None, :]
    slots = jnp.sum(jnp.where(hit, block_slot[None, :], 0), axis=1)
    row_owner, row_local = slots % wide, slots // wide
    col_owner, col_local = slots % narrow, slots // narrow
    row_rank, col_rank = rank_among(row_owner), rank_among(col_owner)
    row_table = spread(row_owner * row_cap + row_rank, row_local, LANES)
    col_table = spread(col_owner * col_cap + col_rank, col_local, LANES)
    far = 1 << 20
    row_blocks = density.shape[0] // BLK
    col_blocks = density.shape[1] // BLK
    row_back = far + spread(
        row_owner * row_blocks + row_local, row_rank * col_cap - far, LANES
    )
    col_back = far + spread(col_owner * col_blocks + col_local, col_rank - far, LANES)
    tile = jnp.stack([row_table, col_table, row_back, col_back] * 2)
    col_place = col_owner * cap + col_rank
    in_plane = row_owner % inner * (narrow * cap) + row_rank * col_cap
    owner_ring = row_owner // inner
    row_in = (ring_me - owner_ring + steps) % steps * (group * cap) + in_plane
    row_out = (ring_me - 1 - owner_ring + 2 * steps) % steps * (group * cap) + in_plane

    tables, rho, moments = gather_density(
        basis_lists,
        row_in,
        col_place,
        point_counts,
        tile,
        weights,
        density,
        orbitals,
        harmonics,
        steps,
        inner,
        narrow,
        (row_cap, col_cap),
    )
    components = harmonics.shape[1]
    total_points = orbitals.shape[0] * orbitals.shape[2] * devices
    parts = integrals(
        basis_lists,
        row_out,
        col_place,
        point_counts,
        orbitals,
        harmonics,
        weights,
        rho,
        moments,
        steps,
        steps * group * cap,
        math.sqrt(total_points * components),
    )
    return return_blocks(
        parts,
        tables,
        density.shape,
        steps,
        inner,
        narrow,
        cap,
    )


def solution(mesh):
    devices = mesh.shape["wide"] * mesh.shape["narrow"]

    def whole(density, block_slot, region_blocks, *others):
        region = region_blocks.shape[0] // devices
        in_specs = (
            P("wide", "narrow"),
            P(),
            P(("wide", "narrow")),
            P(("wide", "narrow"), None),
            P(("wide", "narrow")),
            P(("wide", "narrow"), None, None),
            P(("wide", "narrow"), None),
            P(("wide", "narrow"), None, None),
        )
        mapped = jax.shard_map(
            functools.partial(per_device, region),
            mesh=mesh,
            in_specs=in_specs,
            out_specs=P("wide", "narrow"),
            check_vma=False,
        )
        return mapped(density, block_slot, region_blocks, *others)

    return whole
```
